32 devices in a mesh: patch: 16 (over z, y, x), frame: 2 (over core).
Axes of the slice: x: 2, y: 2, z: 4, core: 2. Of those that a mesh axis runs over, the one named last changes fastest.
Arguments:
- basis: bfloat16 [3, 4096, 1024], P(None, 'patch'), may hold values from -0.25 to 0.25
- latents: bfloat16 [1024, 1024], P('frame', 'patch'), may hold values from -2 to 2
- rest_pos: float32 [3, 4096], P(None, 'patch'), may hold values from -3 to 3
- triangles: int32 [3, 8192], P(None, 'patch'), may hold values from 0 to 511
- hinges: int32 [4, 6144], P(None, 'patch'), may hold values from 0 to 511
- rest_sq: float32 [3, 8192], P(None, 'patch'), may hold values from 0.5 to 3
- bend_rest: float32 [3, 6144], P(None, 'patch'), may hold values from -5 to 5
- masses: float32 [4096], P('patch'), may hold values from 0.5 to 2
- send_rows: int32 [2, 2048], P(None, 'patch'), may hold values from 0 to 255, as said below
Outputs:
- basis_grad: float32 [3, 4096, 1024], P(None, ('patch', 'frame'))
- latent_grad: float32 [1024, 1024], P('frame', 'patch')
The draws below stay inside these ranges and needn't reach their ends.
Inputs may be any that keep to these rules, and one draw needn't show every extreme that they name: `send_rows`: within one patch's columns the 256 entries of both rows are distinct own vertex numbers.
All inputs are finite; a program needn't handle non-finite values.
Results may differ from the reference program's by a relative error of at most 0.006.
Values may be sent and summed in bfloat16 or wider, within the bound.
A program may use at most 64 MiB of HBM per device.

```python
import math
import jax
import jax.numpy as jnp
from jax import lax

LATENT = 1024
VDEV = 256
FR_DEV = 512
HALO = 128
VERTS = 4096
FRAMES = 1024
TRIS = 8192
HINGES = 6144
N_PATCH = 16
N_FRAME = 2


def draw_send_rows(key, part):
    keys = jax.random.split(jax.random.fold_in(key, 17), N_PATCH)

    def one_patch(patch_key):
        shuffled = jax.random.permutation(patch_key, VDEV)
        return shuffled[:2 * HALO].reshape(2, HALO)
    chosen = jax.vmap(one_patch)(keys)
    return jnp.transpose(chosen, (1, 0, 2)).reshape(2, N_PATCH * HALO).astype(jnp.int32)


def plant(values, rng, low, high):
    longest = values.shape.index(max(values.shape))
    spots = []
    for shift in (0, 1):
        where = [jax.random.randint(jax.random.fold_in(rng, axis), (), 0, length) for axis, length in enumerate(values.shape)]
        where[longest] = (where[longest] + shift) % values.shape[longest]
        spots.append(tuple(where))
    return values.at[spots[0]].set(low).at[spots[1]].set(high)


def spiked(entries, own_key, source, target, shards_of, factor):
    def block_of(position):
        return (jnp.arange(entries.shape[position]) // (entries.shape[position] // shards_of)).reshape((-1,) + (1,) * (entries.ndim - 1 - position))

    one_side = jax.random.permutation(own_key, shards_of)[block_of(target)]
    second = (block_of(target) + shards_of // 2) % shards_of
    return jnp.where((block_of(source) == one_side) | (block_of(source) == second), factor * entries, entries)


def shard_levels(key, dims, pieces, least, largest):
    loudness, own = 1.0, jax.random.fold_in(key, 6)
    for axis_at, blocks in pieces:
        steps = jnp.exp(jax.random.uniform(jax.random.fold_in(own, axis_at), (blocks,), jnp.float32, least / len(pieces), largest / len(pieces)))
        loudness = loudness * jnp.repeat(steps, dims[axis_at] // blocks).reshape([-1 if axis == axis_at else 1 for axis in range(len(dims))])
    return loudness


def centred(key, extent, width, most, cuts=(), held_as=jnp.bfloat16):
    result = jax.random.normal(key, extent, jnp.float32) * width
    if len(cuts) > 0:
        result = shard_levels(key, extent, cuts, -0.22, 0.18) * result
    return jnp.clip(result, min=-most, max=most).astype(held_as)


def heavy_noise(key, extent, deviation, reach, cuts, heavy, kind=jnp.bfloat16):
    values = deviation * jax.random.normal(key, extent, jnp.float32)
    if cuts:
        values = values * shard_levels(key, extent, cuts, -0.22, 0.18)
    return jnp.clip(spiked(values, jax.random.fold_in(key, 3), *heavy), -reach, reach).astype(kind)


def setup_inputs(seed: int = 0) -> dict:
    splits = jax.random.split(jax.random.key(seed), 10)
    basis = heavy_noise(splits[0], (3, VERTS, LATENT), LATENT ** -0.5, 0.25, ((1, 16),), (1, 2, 16, 2.0))
    latents = centred(splits[1], (FRAMES, LATENT), 0.3, 2.0, ((0, 2), (1, 16)))
    rest_pos = centred(splits[2], (3, VERTS), 0.5, 3.0, ((1, 16),), jnp.float32)
    triangles = plant(jax.random.randint(splits[3], (3, TRIS), 0, VDEV + 2 * HALO), jax.random.fold_in(splits[3], 1), 0, (VDEV + 2 * HALO) - 1).astype(jnp.int32)
    hinges = plant(jax.random.randint(splits[4], (4, HINGES), 0, VDEV + 2 * HALO), jax.random.fold_in(splits[4], 1), 0, (VDEV + 2 * HALO) - 1).astype(jnp.int32)
    rest_sq = jnp.clip(jnp.exp(math.log(3.0) - 1.7917595 * jax.random.uniform(splits[5], (3, TRIS), jnp.float32) ** shard_levels(splits[5], (3, TRIS), ((1, 16),), -0.2, 0.2)), 0.5, 3.0)
    bend_rest = centred(splits[6], (3, HINGES), 1.0, 5.0, ((1, 16),), jnp.float32)
    masses = jnp.clip(jnp.exp(math.log(2.0) - 1.3862944 * jax.random.uniform(splits[7], (VERTS,), jnp.float32) ** shard_levels(splits[7], (VERTS,), ((0, 16),), -0.2, 0.2)), 0.5, 2.0)
    send_rows = draw_send_rows(jax.random.fold_in(splits[9], 71), 0)
    return dict(basis=basis, latents=latents, rest_pos=rest_pos, triangles=triangles, hinges=hinges, rest_sq=rest_sq, bend_rest=bend_rest, masses=masses, send_rows=send_rows)


MEMBRANE = 5.0
BENDING = 5.0
GRAVITY = 40.0

def elastic(points, corners, hinge_ids, rest_sq, bend_rest):
    point_one = points[:, :, corners[0]]
    point_two = points[:, :, corners[1]]
    point_three = points[:, :, corners[2]]
    edge_list = (point_two - point_one, point_three - point_two, point_one - point_three)
    membrane = jnp.float32(0.0)
    for corner_slot in range(3):
        strain = lax.optimization_barrier(jnp.sum(edge_list[corner_slot] * edge_list[corner_slot], axis=1)) - rest_sq[corner_slot]
        membrane = membrane + jnp.sum(strain * strain)
    bending = points[:, :, hinge_ids[2]] + points[:, :, hinge_ids[3]] - points[:, :, hinge_ids[0]] - points[:, :, hinge_ids[1]] - bend_rest
    return MEMBRANE * membrane + BENDING * jnp.sum(bending * bending)

def extend_ids(local_ids, send_rows):
    row_count = local_ids.shape[0]
    grouped = local_ids.reshape(row_count, N_PATCH, -1)
    senders = send_rows.reshape(2, N_PATCH, HALO)
    device_ids = jnp.arange(N_PATCH, dtype=jnp.int32)[None, :, None]
    previous = (device_ids + N_PATCH - 1) % N_PATCH
    following = (device_ids + 1) % N_PATCH
    from_prev = senders[1][previous, jnp.clip(grouped - VDEV, 0, HALO - 1)] + previous * VDEV
    from_next = senders[0][following, jnp.clip(grouped - VDEV - HALO, 0, HALO - 1)] + following * VDEV
    global_ids = jnp.where(grouped < VDEV, grouped + device_ids * VDEV, jnp.where(grouped < VDEV + HALO, from_prev, from_next))
    return global_ids.reshape(row_count, -1).astype(jnp.int32)

def reference(basis, latents, rest_pos, triangles, hinges, rest_sq, bend_rest, masses, send_rows):
    corners = extend_ids(triangles, send_rows)
    hinge_ids = extend_ids(hinges, send_rows)
    flat_basis = basis.reshape(3 * VERTS, LATENT)
    decoded = jnp.dot(latents, flat_basis.T, preferred_element_type=jnp.float32)
    positions = rest_pos[None] + decoded.reshape(FRAMES, 3, VERTS)
    frame_block = min(32, FRAMES)
    stacked = positions.reshape(FRAMES // frame_block, frame_block, 3, VERTS)
    force_fn = jax.grad(elastic)
    grads = lax.map(lambda frames_block: force_fn(frames_block, corners, hinge_ids, rest_sq, bend_rest), stacked)
    grads = grads.reshape(FRAMES, 3, VERTS)
    grads = grads.at[:, 2, :].add(GRAVITY * masses)
    adjoint = (grads / FRAMES).astype(jnp.bfloat16)
    flat_adjoint = adjoint.reshape(FRAMES, 3 * VERTS)
    latent_grad = jnp.dot(flat_adjoint, flat_basis, preferred_element_type=jnp.float32)
    total = jnp.zeros((3 * VERTS, LATENT), jnp.float32)
    for half_index in range(N_FRAME):
        lower = half_index * FR_DEV
        partial_sum = jnp.dot(flat_adjoint[lower:lower + FR_DEV].T, latents[lower:lower + FR_DEV], preferred_element_type=jnp.float32)
        rounded = lax.optimization_barrier(partial_sum.astype(jnp.bfloat16))
        total = total + rounded.astype(jnp.float32)
    return (total.reshape(3, VERTS, LATENT), latent_grad)
```

```python
import functools

import jax
import jax.numpy as jnp
from jax import lax
from jax.experimental import pallas as pl
from jax.experimental.pallas import tpu as pltpu
from jax.sharding import PartitionSpec as P

MEMBRANE = 5.0
BENDING = 5.0
GRAVITY = 40.0
BF = jnp.bfloat16
F32 = jnp.float32


def hot(rows, ids):
    iota = lax.broadcasted_iota(jnp.int32, (rows, ids.shape[0]), 0)
    return (iota == ids[None, :]).astype(F32)


def mm(a, b, dims):
    return lax.dot_general(a, b, (dims, ((), ())), preferred_element_type=F32)


def exact(a, b):
    return jnp.dot(a, b, precision=lax.Precision.HIGHEST, preferred_element_type=F32)


PLANE = 4
MESH_ID = pl.DeviceIdType.MESH
DMA = pltpu.SemaphoreType.DMA


def places(n):
    p = lax.axis_index("patch")
    xnb = p + 1 - 2 * (p % 2)
    ynb = p + 2 - 4 * ((p // 2) % 2)
    return p, p // PLANE, p % PLANE, xnb, ynb


def greet(peers, pos=None):
    bar = pltpu.get_barrier_semaphore()
    if pos is not None:
        pl.semaphore_signal(bar, inc=1, device_id={"frame": 1 - pos}, device_id_type=MESH_ID)
    for q in peers:
        pl.semaphore_signal(bar, inc=1, device_id={"patch": q}, device_id_type=MESH_ID)
    pl.semaphore_wait(bar, len(peers) + (pos is not None))


def send(src, dst, ss, rs, q):
    return pltpu.make_async_remote_copy(
        src_ref=src, dst_ref=dst, send_sem=ss, recv_sem=rs,
        device_id={"patch": q}, device_id_type=MESH_ID,
    )


def gather_kernel(
    n, w, x_ref, b_ref, sel_ref, r_ref, o_ref, d_ref, t_ref, hb, he,
    zs, zr, xs, xr, ys, yr, rs, rr, hds, hdr, fs, fr, qs, qr
):
    hi = n // PLANE
    p, h, lo, xnb, ynb = places(n)
    pos = lax.axis_index("frame")
    lox, loy = xnb % PLANE, ynb % PLANE
    ring = [(p + n - 1) % n, (p + 1) % n]
    bs = [b_ref.at[c] for c in range(3)]
    vs = b_ref.shape[1]
    ff = x_ref.shape[1]
    hs = sel_ref.shape[1] // 4

    def rows(hh, ll):
        return o_ref.at[pl.ds(pl.multiple_of((hh * PLANE + ll) * w, w), w)]

    def half(ref, c, d, which):
        return ref.at[c, pl.ds(pl.multiple_of((2 * d + which) * hs, hs), hs)]

    zpeer = [((h + j) % hi) * PLANE + lo for j in range(hi)]
    greet(zpeer[1:] + [xnb, ynb] + ring, pos)
    order = sorted(range(1, hi), key=lambda j: min(j, hi - j))
    mine = rows(h, lo)
    zc = {j: send(x_ref, mine, zs.at[j], zr.at[j], zpeer[j]) for j in order}
    xc, yc, rc, hc, fc = {}, {}, {}, {}, {}
    xc[0] = send(x_ref, mine, xs.at[0], xr.at[0], xnb)
    yc[0] = send(x_ref, mine, ys.at[0], yr.at[0], ynb)
    xc[0].start()
    yc[0].start()
    for j in reversed(order):
        zc[j].start()
    rest = [send(r_ref.at[d], t_ref.at[1 - d], qs.at[d], qr.at[d], ring[d]) for d in range(2)]
    rest[0].start()
    rest[1].start()

    def halo(c):
        for d in range(2):
            hc[c, d] = send(
                half(hb, c, d, pos), half(he, c, 1 - d, pos),
                hds.at[2 * c + d], hdr.at[2 * c + d], ring[d],
            )
            hc[c, d].start()

    def swap(c):
        for d in range(2):
            hc[c, d].wait_recv()
            part = half(he, c, 1 - d, pos)
            fc[c, d] = pltpu.make_async_remote_copy(
                src_ref=part, dst_ref=part,
                send_sem=fs.at[2 * c + d], recv_sem=fr.at[2 * c + d],
                device_id={"frame": 1 - pos}, device_id_type=MESH_ID,
            )
            fc[c, d].start()

    def decode(c, src, at, count):
        d_ref[at : at + count, c * ff : (c + 1) * ff] = mm(
            src, o_ref[...], ((1,), (0,))
        ).astype(BF)

    def far(c):
        fc[c, 0].wait_recv()
        fc[c, 1].wait_recv()
        decode(c, he[c], vs, 4 * hs)

    for c in range(3):
        hb[c] = mm(sel_ref[...], bs[c][...], ((0,), (0,))).astype(BF)
        if c == 0:
            halo(0)
    mine[...] = x_ref[...]

    def relay(j):
        hh = (h + hi - j) % hi
        xc[j].wait_recv()
        part = rows(hh, lox)
        rc[j] = send(part, part, rs.at[j], rr.at[j], ynb)
        rc[j].start()

    last = 0
    for at, j in enumerate(order):
        zc[j].wait_recv()
        part = rows((h + hi - j) % hi, lo)
        xc[j] = send(part, part, xs.at[j], xr.at[j], xnb)
        yc[j] = send(part, part, ys.at[j], yr.at[j], ynb)
        xc[j].start()
        yc[j].start()
        if at == 1:
            halo(1)
        relay(last)
        last = j
    if len(order) < 2:
        halo(1)
    relay(last)
    halo(2)
    for j in range(hi):
        yc[j].wait_recv()
        rc[j].wait_recv()
    swap(0)
    for c in range(3):
        decode(c, bs[c][...], 0, vs)
    swap(1)
    far(0)
    swap(2)
    far(1)
    far(2)
    for d in range(2):
        rest[d].wait_recv()
        rest[d].wait_send()
    for c in range(3):
        for d in range(2):
            fc[c, d].wait_send()
            hc[c, d].wait_send()
    for j in range(hi):
        if j:
            zc[j].wait_send()
        xc[j].wait_send()
        yc[j].wait_send()
        rc[j].wait_send()


def gather_all(x, basis, sel, rsend, n):
    w, f = x.shape
    hi = n // PLANE
    _, vs, kk = basis.shape
    slots = sel.shape[1]
    vm = pl.BlockSpec(memory_space=pltpu.VMEM)
    return pl.pallas_call(
        functools.partial(gather_kernel, n, w),
        out_shape=[
            jax.ShapeDtypeStruct((n * w, f), x.dtype),
            jax.ShapeDtypeStruct((vs + slots, 3 * f), x.dtype),
            jax.ShapeDtypeStruct(rsend.shape, rsend.dtype),
        ],
        in_specs=[vm] * 4,
        out_specs=[vm] * 3,
        scratch_shapes=[pltpu.VMEM((3, slots, kk), x.dtype)] * 2
        + [DMA((hi,))] * 8 + [DMA((6,))] * 4 + [DMA((2,))] * 2,
        compiler_params=pltpu.CompilerParams(
            collective_id=0, has_side_effects=True, vmem_limit_bytes=16000 * 1024
        ),
    )(x, basis, sel, rsend)


def tail_kernel(
    n, w, own_ref, gh_ref, sel_ref, b_ref, lt_ref, lo_ref, bg_ref, o_ref,
    bt, bk, adj, got, acc, g, rl, sb, cx, cy, zb, zl,
    ks, kr, ps, pr, ls, lr, xs, xr, ys, yr, zs, zr,
):
    hi = n // PLANE
    p, h, lo, xnb, ynb = places(n)
    pos = lax.axis_index("frame")
    lox, loy = xnb % PLANE, ynb % PLANE
    lod = PLANE - 1 - lo
    ring = [(p + n - 1) % n, (p + 1) % n]
    bs = [b_ref.at[c] for c in range(3)]
    _, vs, kk = b_ref.shape
    ff = lt_ref.shape[1]
    halo = gh_ref.shape[0] // 2
    half = vs // 2
    tile = 256

    def rows(j, ll):
        hh = (h + j) % hi
        return g.at[pl.ds(pl.multiple_of((hh * PLANE + ll) * w, w), w)]

    zpeer = [((h + j) % hi) * PLANE + lo for j in range(hi)]
    greet(zpeer[1:] + [xnb, ynb] + ring, pos)
    kc, pc = {}, []
    for c in range(3):
        for d in range(2):
            kc[c, d] = send(
                gh_ref.at[pl.ds(d * halo, halo), pl.ds(c * ff, ff)],
                bk.at[c, pl.ds((1 - d) * halo, halo)],
                ks.at[2 * c + d], kr.at[2 * c + d], ring[d],
            )
            kc[c, d].start()
    for c in range(3):
        bt[c] = bs[c][...].T
    for c in range(3):
        kc[c, 0].wait_recv()
        kc[c, 1].wait_recv()
        adj[c] = (
            own_ref[:, pl.ds(c * ff, ff)] + mm(sel_ref[...], bk[c], ((1,), (0,)))
        ).astype(BF)
        cp = pltpu.make_async_remote_copy(
            src_ref=adj.at[c, pl.ds(pl.multiple_of((1 - pos) * half, half), half)],
            dst_ref=got.at[c], send_sem=ps.at[c], recv_sem=pr.at[c],
            device_id={"frame": 1 - pos}, device_id_type=MESH_ID,
        )
        cp.start()
        pc.append(cp)
        for r in range(0, kk, tile):
            block = mm(bt[c, r : r + tile], adj[c], ((1,), (0,)))
            if c:
                block = block + acc[r : r + tile]
            if c < 2:
                acc[r : r + tile] = block
            else:
                g[r : r + tile] = block.astype(BF)

    def grad(c):
        mine = adj[c, pl.ds(pl.multiple_of(pos * half, half), half)]
        for r in range(0, kk, tile):
            bg_ref[0, c, :, r : r + tile] = mm(mine, lt_ref[r : r + tile], ((1,), (1,))).astype(BF)
            bg_ref[1, c, :, r : r + tile] = mm(got[c], lo_ref[r : r + tile], ((1,), (1,))).astype(BF)

    order = sorted(range(1, hi), key=lambda j: -min(j, hi - j))
    lc, xc, yc, zc = {}, {}, {}, {}

    def via(j):
        lc[j] = send(rows(j, lod), rl.at[j], ls.at[j], lr.at[j], ynb)
        lc[j].start()

    def to_x(j, src):
        xc[j] = send(src, cx.at[j], xs.at[j], xr.at[j], xnb)
        xc[j].start()

    def to_y(j, src):
        yc[j] = send(src, cy.at[j], ys.at[j], yr.at[j], ynb)
        yc[j].start()

    def summed(j):
        lc[j].wait_recv()
        own = rows(j, lox)
        sb[j] = (own[...].astype(F32) + rl[j].astype(F32)).astype(BF)
        to_x(j, sb.at[j])

    def total(j):
        xc[j].wait_recv()
        yc[j].wait_recv()
        return rows(j, lo)[...].astype(F32) + cx[j].astype(F32) + cy[j].astype(F32)

    for j in order:
        via(j)
        to_y(j, rows(j, loy))
    for c in range(3):
        pc[c].wait_recv()
    grad(0)
    for j in order:
        summed(j)
    via(0)
    to_y(0, rows(0, loy))
    grad(1)
    for j in order:
        zb[j] = total(j).astype(BF)
        zc[j] = send(zb.at[j], zl.at[j], zs.at[j], zr.at[j], zpeer[j])
        zc[j].start()
    summed(0)
    grad(2)
    s = total(0)
    for j in reversed(order):
        zc[j].wait_recv()
        s = s + zl[j].astype(F32)
    o_ref[...] = s
    for c in range(3):
        kc[c, 0].wait_send()
        kc[c, 1].wait_send()
        pc[c].wait_send()
    for j in [0] + order:
        lc[j].wait_send()
        xc[j].wait_send()
        yc[j].wait_send()
        if j:
            zc[j].wait_send()


def tail(own, gh, sel, basis, lat_t, lat_o, n):
    kk, f = lat_t.shape
    w = kk // n
    hi = n // PLANE
    vs = own.shape[0]
    vm = pl.BlockSpec(memory_space=pltpu.VMEM)
    vmem = pltpu.VMEM
    return pl.pallas_call(
        functools.partial(tail_kernel, n, w),
        out_shape=[
            jax.ShapeDtypeStruct((2, 3, vs // 2, kk), BF),
            jax.ShapeDtypeStruct((w, f), F32),
        ],
        in_specs=[vm] * 6,
        out_specs=[vm] * 2,
        scratch_shapes=[
            vmem((3, kk, vs), BF),
            vmem((3, gh.shape[0], f), BF),
            vmem((3, vs, f), BF),
            vmem((3, vs // 2, f), BF),
            vmem((kk, f), F32),
            vmem((kk, f), BF),
        ]
        + [vmem((hi, w, f), BF)] * 6
        + [DMA((6,))] * 2
        + [DMA((3,))] * 2
        + [DMA((hi,))] * 8,
        compiler_params=pltpu.CompilerParams(
            collective_id=1, has_side_effects=True, vmem_limit_bytes=24000 * 1024
        ),
    )(own, gh, sel, basis, lat_t, lat_o)


def local(basis, latents, rest_pos, triangles, hinges, rest_sq, bend_rest, masses, send_rows):
    vs = basis.shape[1]
    ff = latents.shape[0]
    halo = send_rows.shape[1]
    nt = triangles.shape[1]
    total = ff * lax.axis_size("frame")
    pos = lax.axis_index("frame")
    n = lax.axis_size("patch")
    ext = vs + 2 * halo
    ta, tb, tc = (hot(ext, triangles[i]) for i in range(3))
    ha, hb, hc, hd = (hot(ext, hinges[i]) for i in range(4))
    inc = jnp.concatenate([tb - ta, tc - tb, hc + hd - ha - hb], axis=1).astype(BF)
    self32 = hot(vs, send_rows.reshape(-1))
    sel = self32.astype(BF)
    rest_out = exact(rest_pos, self32)
    rsend = jnp.pad(rest_out.reshape(3, 2, halo).transpose(1, 0, 2), ((0, 0), (0, 5), (0, 0)))
    lat_t, dext, rhalo = gather_all(latents.T, basis, sel, rsend, n)
    lat_o = lax.ppermute(lat_t, "frame", [(0, 1), (1, 0)])
    rest_ext = jnp.concatenate([rest_pos, rhalo[0, :3], rhalo[1, :3]], axis=1)
    rest_edge = exact(rest_ext, inc.astype(F32))
    rest_edge = rest_edge.at[:, 2 * nt :].add(-bend_rest)
    edges = mm(inc, dext, ((0,), (0,)))
    e1 = [edges[:nt, c * ff : (c + 1) * ff] + rest_edge[c, :nt, None] for c in range(3)]
    e2 = [edges[nt : 2 * nt, c * ff : (c + 1) * ff] + rest_edge[c, nt : 2 * nt, None] for c in range(3)]
    hh = [edges[2 * nt :, c * ff : (c + 1) * ff] + rest_edge[c, 2 * nt :, None] for c in range(3)]
    e3 = [-(a + b) for a, b in zip(e1, e2)]
    k = 4.0 * MEMBRANE / total

    def strain(e, r):
        return k * (e[0] * e[0] + e[1] * e[1] + e[2] * e[2] - r[:, None])

    s1, s2, s3 = strain(e1, rest_sq[0]), strain(e2, rest_sq[1]), strain(e3, rest_sq[2])
    u1 = jnp.concatenate([s1 * e1[c] - s3 * e3[c] for c in range(3)], axis=1)
    u2 = jnp.concatenate([s2 * e2[c] - s3 * e3[c] for c in range(3)], axis=1)
    uh = jnp.concatenate(hh, axis=1) * (2.0 * BENDING / total)
    forces = jnp.concatenate([u1, u2, uh], axis=0).astype(BF)
    g = mm(inc, forces, ((1,), (0,)))
    gh = g[vs:].astype(BF)
    owned = g[:vs].at[:, 2 * ff :].add((GRAVITY / total) * masses[:, None])
    halves, lg = tail(owned, gh, sel, basis, lat_t, lat_o, n)
    return (halves[0].astype(F32) + halves[1].astype(F32), lg.T)


def solution(mesh):
    return jax.shard_map(
        local,
        mesh=mesh,
        in_specs=(
            P(None, "patch", None),
            P("frame", "patch"),
            P(None, "patch"),
            P(None, "patch"),
            P(None, "patch"),
            P(None, "patch"),
            P(None, "patch"),
            P("patch"),
            P(None, "patch"),
        ),
        out_specs=(P(None, ("patch", "frame"), None), P("frame", "patch")),
        check_vma=False,
    )
```

```python
import functools

import jax
import jax.numpy as jnp
from jax import lax
from jax.experimental import pallas as pl
from jax.experimental.pallas import tpu as pltpu
from jax.sharding import PartitionSpec as P

MEMBRANE = 5.0
BENDING = 5.0
GRAVITY = 40.0
BF = jnp.bfloat16
F32 = jnp.float32
PLANE = 4
LANES = 128
CHUNKS = 2
MESH_ID = pl.DeviceIdType.MESH
DMA = pltpu.SemaphoreType.DMA


def mm(a, b, dims=((1,), (0,))):
    return lax.dot_general(a, b, (dims, ((), ())), preferred_element_type=F32)


NT = ((1,), (1,))
TN = ((0,), (0,))


def split3(r):
    hi = r.astype(BF)
    left = r - hi.astype(F32)
    mid = left.astype(BF)
    return hi, mid, (left - mid.astype(F32)).astype(BF)


def send(src, dst, ss, rs, q):
    return pltpu.make_async_remote_copy(
        src_ref=src, dst_ref=dst, send_sem=ss, recv_sem=rs,
        device_id={"patch": q}, device_id_type=MESH_ID,
    )


def column(row):
    return jnp.broadcast_to(row, (LANES, row.shape[1])).T


def kernel(
    n, frames,
    x_hbm, b_hbm, rest_hbm, tri_hbm, hin_hbm, rsq_hbm, bend_hbm, mass_hbm, rows_hbm,
    bg_ref, lg_ref,
    xs, xo, be, bet, hb, tri, hin, rsq, bend, mass, rows, restb, restx, sel, inc, inct,
    rb, sq, bd, mb, dec, edge, force, adj, own, bk, tot, got, g, yl, ysum, zl, xsum, xl,
    ins, xsem, ysem, zsem, rsem, hsem, wsem, osem, ksem, psem, ry, rz, rx,
):
    hi = n // PLANE
    w = x_hbm.shape[0]
    p = lax.axis_index("patch")
    pos = lax.axis_index("frame")
    h, lo = p // PLANE, p % PLANE
    xnb = p + 1 - 2 * (p % 2)
    ynb = p + 2 - 4 * ((p // 2) % 2)
    lox, loy, lod = xnb % PLANE, ynb % PLANE, PLANE - 1 - lo
    ring = [(p + n - 1) % n, (p + 1) % n]
    vs, kk = b_hbm.shape[1:]
    ff = x_hbm.shape[1]
    halo = rows_hbm.shape[1]
    ext = vs + 2 * halo
    hs = halo // 2
    nt, nh = tri_hbm.shape[1], hin_hbm.shape[1]
    half = vs // 2
    pc = ff // CHUNKS
    tile = 256

    def partner(src, dst, sems, at):
        return pltpu.make_async_remote_copy(
            src_ref=src, dst_ref=dst, send_sem=sems.at[0, at], recv_sem=sems.at[1, at],
            device_id={"frame": 1 - pos}, device_id_type=MESH_ID,
        )

    out = []

    def go(src, dst, sems, at, q):
        c = send(src, dst, sems.at[0, at], sems.at[1, at], q)
        c.start()
        out.append(c)
        return c

    def cross(src, dst, sems, at):
        c = partner(src, dst, sems, at)
        c.start()
        out.append(c)
        return c

    small = [(rows_hbm, rows), (rest_hbm, restb), (tri_hbm, tri), (hin_hbm, hin),
             (rsq_hbm, rsq), (bend_hbm, bend), (mass_hbm, mass)]
    ends = [(s, d) for s, d in small[:2]]
    ends += [(b_hbm.at[c], be.at[c, pl.ds(0, vs)]) for c in range(3)]
    ends += small[2:]
    fetch = [pltpu.make_async_copy(s, d, ins.at[i]) for i, (s, d) in enumerate(ends)]
    for f in fetch:
        f.start()

    zpeer = [((h + j) % hi) * PLANE + lo for j in range(hi)]

    def row(hh, ll):
        return xs.at[pl.ds(pl.multiple_of((hh * PLANE + ll) * w, w), w)]

    mine = row(h, lo)
    keep = pltpu.make_async_copy(x_hbm, mine, ins.at[len(ends)])
    keep.start()

    bar = pltpu.get_barrier_semaphore()
    pl.semaphore_signal(bar, inc=1, device_id={"frame": 1 - pos}, device_id_type=MESH_ID)
    peers = zpeer[1:] + [xnb, ynb] + ring
    for q in peers:
        pl.semaphore_signal(bar, inc=1, device_id={"patch": q}, device_id_type=MESH_ID)
    pl.semaphore_wait(bar, len(peers) + 1)

    order = sorted(range(1, hi), key=lambda j: -min(j, hi - j))
    near = order[::-1]
    xc = go(x_hbm, mine, xsem, 0, xnb)
    za, zb, ya, yb = {}, {}, {}, {}
    for j in order:
        za[j] = go(x_hbm, mine, zsem, j, zpeer[j])
    ya[0] = go(x_hbm, mine, ysem, 0, ynb)

    def hot(count, ids, dtype):
        iota = lax.broadcasted_iota(jnp.int32, (count, ids.shape[1]), 0)
        return jnp.where(iota == ids, 1.0, 0.0).astype(dtype)

    fetch[0].wait()
    fetch[1].wait()
    for d in range(2):
        sel[:, d * halo : (d + 1) * halo] = hot(vs, rows[d : d + 1], BF)
    parts = split3(restb[...])
    sent = sum(mm(part, sel[...]) for part in parts)
    rc = []
    for d in range(2):
        restx[d] = sent[:, d * halo : (d + 1) * halo]
        rc.append(go(restx.at[d], restx.at[3 - d], rsem, d, ring[d]))

    hc, fc = {}, {}

    def part_of(ref, base, c, d):
        at = pl.multiple_of(base + d * halo + pos * hs, hs)
        return ref.at[c, pl.ds(at, hs)]

    for c in range(3):
        fetch[2 + c].wait()
        hb[c] = mm(sel[...], be[c, 0:vs], TN).astype(BF)
        for d in range(2):
            hc[c, d] = go(
                part_of(hb, 0, c, d), part_of(be, vs, c, 1 - d), hsem, 2 * c + d, ring[d]
            )
        if c == 0:
            xc.wait_recv()
            side = row(h, lox)
            for j in order:
                zb[j] = go(side, side, zsem, hi + j, zpeer[j])
            yb[0] = go(side, side, ysem, hi, ynb)

    def relay(j):
        hh = (h + hi - j) % hi
        za[j].wait_recv()
        part = row(hh, lo)
        ya[j] = go(part, part, ysem, j, ynb)

    def relay_side(j):
        hh = (h + hi - j) % hi
        zb[j].wait_recv()
        part = row(hh, lox)
        yb[j] = go(part, part, ysem, hi + j, ynb)

    def swap(c):
        for d in range(2):
            hc[c, d].wait_recv()
            part = part_of(be, vs, c, 1 - d)
            fc[c, d] = cross(part, part, wsem, 2 * c + d)

    for f in fetch[5:]:
        f.wait()

    def corner(ref, i, at, count):
        return hot(ext, ref[i : i + 1, at : at + count], F32)

    def build(at, count, plus, minus):
        total = None
        for ref, i, begin in plus:
            one = corner(ref, i, begin, count)
            total = one if total is None else total + one
        for ref, i, begin in minus:
            total = total - corner(ref, i, begin, count)
        inc[:, at : at + count] = total.astype(BF)
        inct[at : at + count] = inc[:, at : at + count].T

    def build_edges(i):
        for b in range(0, nt, LANES):
            build(i * nt + b, LANES, [(tri, i + 1, b)], [(tri, i, b)])

    for j in near:
        relay(j)
    build_edges(0)
    for j in near:
        relay_side(j)
    build_edges(1)
    for b in range(0, nh, LANES):
        build(
            2 * nt + b, LANES, [(hin, 2, b), (hin, 3, b)], [(hin, 0, b), (hin, 1, b)]
        )
    swap(0)
    keep.wait()

    for i in range(3):
        sq[i] = column(rsq[i : i + 1])
        bd[i] = column(bend[i : i + 1])
    mb[...] = column(mass[...])
    for d in range(2):
        rc[d].wait_recv()
    for c in range(3):
        line = jnp.concatenate(
            [restb[c : c + 1], restx[2, c : c + 1], restx[3, c : c + 1]], axis=1
        )
        cols = sum(
            mm(inct[...], jnp.broadcast_to(part, (LANES, ext)), NT) for part in split3(line)
        )
        rb[c, 0 : 2 * nt] = cols[0 : 2 * nt]
        rb[c, 2 * nt :] = cols[2 * nt :] - bd[c]
    for c in range(3):
        bet[:, c * ext : c * ext + vs] = be[c, 0:vs].T

    for j in range(hi):
        ya[j].wait_recv()
        yb[j].wait_recv()

    def decode(c, at, count, lanes):
        dec[c, at : at + count, lanes] = mm(be[c, at : at + count], xs[:, lanes]).astype(BF)

    def stretch(c, lanes):
        for r in range(0, 2 * nt + nh, 352):
            edge[c, r : r + 352, lanes] = mm(inct[r : r + 352], dec[c, :, lanes])

    every = pl.ds(0, ff)
    for c in range(3):
        decode(c, 0, vs, every)
        if c == 0:
            swap(1)
    for c in range(2):
        for d in range(2):
            fc[c, d].wait_recv()
        decode(c, vs, 2 * halo, every)
        stretch(c, every)
        bet[:, c * ext + vs : (c + 1) * ext] = be[c, vs:ext].T
    swap(2)
    oc = cross(xs, xo, osem, 0)
    for d in range(2):
        fc[2, d].wait_recv()

    k = 4.0 * MEMBRANE / frames
    kc, yc, pcs = {}, {}, {}

    def elastic(q):
        step = 16

        def body(i, carry):
            r = pl.multiple_of(i * step, step)
            for t in range(0, pc, LANES):
                lanes = pl.ds(q * pc + t, LANES)
                e1 = [edge[c, pl.ds(r, step), lanes] + rb[c, pl.ds(r, step)] for c in range(3)]
                r2 = pl.multiple_of(nt + r, step)
                e2 = [edge[c, pl.ds(r2, step), lanes] + rb[c, pl.ds(r2, step)] for c in range(3)]
                e3 = [a + b for a, b in zip(e1, e2)]

                def strain(e, i):
                    return e[0] * e[0] + e[1] * e[1] + e[2] * e[2] - sq[i, pl.ds(r, step)]

                s1, s2, s3 = strain(e1, 0), strain(e2, 1), strain(e3, 2)
                for c in range(3):
                    u = s3 * e3[c]
                    force[c, pl.ds(r, step), pl.ds(t, LANES)] = (s1 * e1[c] + u).astype(BF)
                    force[c, pl.ds(r2, step), pl.ds(t, LANES)] = (s2 * e2[c] + u).astype(BF)
            return carry

        lax.fori_loop(0, nt // step, body, 0)

        def bend_body(i, carry):
            r = pl.multiple_of(2 * nt + i * step, step)
            for c in range(3):
                for t in range(0, pc, LANES):
                    e = edge[c, pl.ds(r, step), pl.ds(q * pc + t, LANES)] + rb[c, pl.ds(r, step)]
                    force[c, pl.ds(r, step), pl.ds(t, LANES)] = (
                        e * (0.5 * BENDING / MEMBRANE)
                    ).astype(BF)
            return carry

        lax.fori_loop(0, nh // step, bend_body, 0)

    for q in range(CHUNKS):
        lanes = pl.ds(q * pc, pc)
        decode(2, vs, 2 * halo, lanes)
        stretch(2, lanes)
        elastic(q)
        for c in range(3):
            adj[q, c * ext + vs : (c + 1) * ext] = (mm(inc[vs:ext], force[c]) * k).astype(BF)
            for d in range(2):
                kc[q, c, d] = go(
                    adj.at[q, pl.ds(c * ext + vs + d * halo, halo)],
                    bk.at[q, c, pl.ds((1 - d) * halo, halo)],
                    ksem, (q * 3 + c) * 2 + d, ring[d],
                )
        for c in range(3):
            part = mm(inc[0:vs], force[c]) * k
            if c == 2:
                lift = mb[...] * (GRAVITY / frames)
                part = part + jnp.concatenate([lift] * (pc // LANES), axis=1)
            own[q, c] = part
            adj[q, c * ext : c * ext + vs] = part.astype(BF)
        if q == 0:
            bet[:, 2 * ext + vs : 3 * ext] = be[2, vs:ext].T
        for r in range(0, kk, tile):
            g[q, r : r + tile] = mm(bet[r : r + tile], adj[q]).astype(BF)
        for j in order + [0]:
            hh = (h + j) % hi
            for i, ll in enumerate((loy, lod)):
                at = pl.multiple_of((hh * PLANE + ll) * w, w)
                yc[q, j, i] = go(
                    g.at[q, pl.ds(at, w)], yl.at[q, j, i], ry, (q * hi + j) * 2 + i, ynb
                )

    def fold(q, j, i):
        hh = (h + j) % hi
        at = pl.multiple_of((hh * PLANE + (lox if i else lo)) * w, w)
        yc[q, j, i].wait_recv()
        return g[q, pl.ds(at, w)].astype(F32) + yl[q, j, i].astype(F32)

    zc = {}

    def depth(q):
        for j in order:
            for i in range(2):
                ysum[q, j, i] = fold(q, j, i).astype(BF)
                zc[q, j, i] = go(
                    ysum.at[q, j, i], zl.at[q, j, i], rz, (q * hi + j) * 2 + i, zpeer[j]
                )

    held = {}

    def gather_z(q, i):
        s = fold(q, 0, i)
        for j in order:
            zc[q, j, i].wait_recv()
            s = s + zl[q, j, i].astype(F32)
        return s

    def collect(q):
        for c in range(3):
            kc[q, c, 0].wait_recv()
            kc[q, c, 1].wait_recv()
            tot[c, :, q * pc : (q + 1) * pc] = (own[q, c] + mm(sel[...], bk[q, c])).astype(BF)
            theirs = pl.ds(pl.multiple_of((1 - pos) * half, half), half)
            pcs[q, c] = cross(
                tot.at[c, theirs, pl.ds(q * pc, pc)], got.at[c, :, pl.ds(q * pc, pc)],
                psem, q * 3 + c,
            )

    rxc = {}

    def turn(q):
        xsum[q] = gather_z(q, 1).astype(BF)
        rxc[q] = go(xsum.at[q], xl.at[q], rx, q, xnb)

    def finish(q):
        s = gather_z(q, 0)
        rxc[q].wait_recv()
        lg_ref[:, q * pc : (q + 1) * pc] = s + xl[q].astype(F32)

    def product(which, src, lat, c):
        for r in range(0, kk, tile):
            bg_ref[which, c, :, r : r + tile] = mm(src, lat[r : r + tile], NT).astype(BF)

    for q in range(CHUNKS):
        depth(q)
    for q in range(CHUNKS - 1):
        collect(q)
    for q in range(CHUNKS):
        turn(q)
    collect(CHUNKS - 1)
    for c in range(3):
        product(0, tot[c, pl.ds(pl.multiple_of(pos * half, half), half)], xs, c)
    oc.wait_recv()
    for c in range(3):
        for q in range(CHUNKS):
            pcs[q, c].wait_recv()
        product(1, got[c], xo, c)
    for q in range(CHUNKS):
        finish(q)
    for c in out:
        c.wait_send()


def local(basis, latents, rest_pos, triangles, hinges, rest_sq, bend_rest, masses, send_rows):
    vs, kk = basis.shape[1:]
    ff, w = latents.shape
    halo = send_rows.shape[1]
    nt, nh = triangles.shape[1], hinges.shape[1]
    n = lax.axis_size("patch")
    hi = n // PLANE
    frames = ff * lax.axis_size("frame")
    ext = vs + 2 * halo
    ne = 2 * nt + nh
    pc = ff // CHUNKS
    v = pltpu.VMEM
    i32 = jnp.int32
    vm = pl.BlockSpec(memory_space=pltpu.VMEM)
    hbm = pl.BlockSpec(memory_space=pltpu.HBM)
    halves, lg = pl.pallas_call(
        functools.partial(kernel, n, frames),
        out_shape=[
            jax.ShapeDtypeStruct((2, 3, vs // 2, kk), BF),
            jax.ShapeDtypeStruct((w, ff), F32),
        ],
        in_specs=[hbm] * 9,
        out_specs=[vm] * 2,
        scratch_shapes=[
            v((kk, ff), BF),
            v((kk, ff), BF),
            v((3, ext, kk), BF),
            v((kk, 3 * ext), BF),
            v((3, 2 * halo, kk), BF),
            v((3, nt), i32),
            v((4, nh), i32),
            v((3, nt), F32),
            v((3, nh), F32),
            v((1, vs), F32),
            v((2, halo), i32),
            v((3, vs), F32),
            v((4, 3, halo), F32),
            v((vs, 2 * halo), BF),
            v((ext, ne), BF),
            v((ne, ext), BF),
            v((3, ne, LANES), F32),
            v((3, nt, LANES), F32),
            v((3, nh, LANES), F32),
            v((vs, LANES), F32),
            v((3, ext, ff), BF),
            v((3, ne, ff), F32),
            v((3, ne, pc), BF),
            v((CHUNKS, 3 * ext, pc), BF),
            v((CHUNKS, 3, vs, pc), F32),
            v((CHUNKS, 3, 2 * halo, pc), BF),
            v((3, vs, ff), BF),
            v((3, vs // 2, ff), BF),
            v((CHUNKS, kk, pc), BF),
            v((CHUNKS, hi, 2, w, pc), BF),
            v((CHUNKS, hi, 2, w, pc), BF),
            v((CHUNKS, hi, 2, w, pc), BF),
            v((CHUNKS, w, pc), BF),
            v((CHUNKS, w, pc), BF),
            DMA((11,)),
            DMA((2, 1)),
            DMA((2, 2 * hi)),
            DMA((2, 2 * hi)),
            DMA((2, 2)),
            DMA((2, 6)),
            DMA((2, 6)),
            DMA((2, 1)),
            DMA((2, CHUNKS * 6)),
            DMA((2, CHUNKS * 3)),
            DMA((2, CHUNKS * hi * 2)),
            DMA((2, CHUNKS * hi * 2)),
            DMA((2, CHUNKS)),
        ],
        compiler_params=pltpu.CompilerParams(
            collective_id=0, has_side_effects=True, vmem_limit_bytes=52000 * 1024
        ),
    )(
        latents.T, basis, rest_pos, triangles, hinges, rest_sq, bend_rest,
        masses.reshape(1, vs), send_rows,
    )
    return (halves[0].astype(F32) + halves[1].astype(F32), lg.T)


def solution(mesh):
    return jax.shard_map(
        local,
        mesh=mesh,
        in_specs=(
            P(None, "patch", None),
            P("frame", "patch"),
            P(None, "patch"),
            P(None, "patch"),
            P(None, "patch"),
            P(None, "patch"),
            P(None, "patch"),
            P("patch"),
            P(None, "patch"),
        ),
        out_specs=(P(None, ("patch", "frame"), None), P("frame", "patch")),
        check_vma=False,
    )
```

```python
import functools

import jax
import jax.numpy as jnp
from jax import lax
from jax.experimental import pallas as pl
from jax.experimental.pallas import tpu as pltpu
from jax.sharding import PartitionSpec as P

MEMBRANE = 5.0
BENDING = 5.0
GRAVITY = 40.0
BF = jnp.bfloat16
F32 = jnp.float32
PLANE = 4
LANES = 128
CHUNKS = 2
MESH_ID = pl.DeviceIdType.MESH
DMA = pltpu.SemaphoreType.DMA


def mm(a, b, dims=((1,), (0,))):
    return lax.dot_general(a, b, (dims, ((), ())), preferred_element_type=F32)


NT = ((1,), (1,))
TN = ((0,), (0,))


def split3(r):
    hi = r.astype(BF)
    left = r - hi.astype(F32)
    mid = left.astype(BF)
    return hi, mid, (left - mid.astype(F32)).astype(BF)


def send(src, dst, ss, rs, q):
    return pltpu.make_async_remote_copy(
        src_ref=src, dst_ref=dst, send_sem=ss, recv_sem=rs,
        device_id={"patch": q}, device_id_type=MESH_ID,
    )


def column(row):
    return jnp.broadcast_to(row, (LANES, row.shape[1])).T


def kernel(
    n, frames,
    x_hbm, b_hbm, rest_hbm, tri_hbm, hin_hbm, rsq_hbm, bend_hbm, mass_hbm, rows_hbm,
    bg_ref, lg_ref,
    xs, xo, be, bet, hb, tri, hin, rsq, bend, mass, rows, restb, restx, sel, inc, inct,
    rb, sq, bd, mb, dec, edge, force, adj, own, bk, tot, got, g, yl, ysum, zl, xsum, xl,
    ins, xsem, ysem, zsem, rsem, hsem, wsem, osem, ksem, psem, ry, rz, rx,
):
    hi = n // PLANE
    w = x_hbm.shape[0]
    p = lax.axis_index("patch")
    pos = lax.axis_index("frame")
    h, lo = p // PLANE, p % PLANE
    xnb = p + 1 - 2 * (p % 2)
    ynb = p + 2 - 4 * ((p // 2) % 2)
    lox, loy, lod = xnb % PLANE, ynb % PLANE, PLANE - 1 - lo
    odd = p % 2
    toward = [xnb, (p + n - 1 + 2 * odd) % n]
    slot = [1 - odd, odd]
    ring = [(p + n - 1) % n, (p + 1) % n]
    vs, kk = b_hbm.shape[1:]
    ff = x_hbm.shape[1]
    halo = rows_hbm.shape[1]
    ext = vs + 2 * halo
    hs = halo // 2
    nt, nh = tri_hbm.shape[1], hin_hbm.shape[1]
    half = vs // 2
    pc = ff // CHUNKS
    tile = 256

    def partner(src, dst, sems, at):
        return pltpu.make_async_remote_copy(
            src_ref=src, dst_ref=dst, send_sem=sems.at[0, at], recv_sem=sems.at[1, at],
            device_id={"frame": 1 - pos}, device_id_type=MESH_ID,
        )

    out = []

    def go(src, dst, sems, at, q):
        c = send(src, dst, sems.at[0, at], sems.at[1, at], q)
        c.start()
        out.append(c)
        return c

    def cross(src, dst, sems, at):
        c = partner(src, dst, sems, at)
        c.start()
        out.append(c)
        return c

    small = [(rows_hbm, rows), (rest_hbm, restb), (tri_hbm, tri), (hin_hbm, hin),
             (rsq_hbm, rsq), (bend_hbm, bend), (mass_hbm, mass)]
    ends = [(s, d) for s, d in small[:2]]
    ends += [(b_hbm.at[c], be.at[c, pl.ds(0, vs)]) for c in range(3)]
    ends += small[2:]
    fetch = [pltpu.make_async_copy(s, d, ins.at[i]) for i, (s, d) in enumerate(ends)]
    for f in fetch:
        f.start()

    zpeer = [((h + j) % hi) * PLANE + lo for j in range(hi)]

    def row(hh, ll, q):
        at = pl.multiple_of((hh * PLANE + ll) * w, w)
        return xs.at[pl.ds(at, w), pl.ds(q * pc, pc)]

    def source(q):
        return x_hbm.at[:, pl.ds(q * pc, pc)]

    keep = pltpu.make_async_copy(
        x_hbm, xs.at[pl.ds(pl.multiple_of(p * w, w), w)], ins.at[len(ends)]
    )
    keep.start()

    bar = pltpu.get_barrier_semaphore()
    pl.semaphore_signal(bar, inc=1, device_id={"frame": 1 - pos}, device_id_type=MESH_ID)
    peers = zpeer[1:] + [xnb, ynb] + ring
    for q in peers:
        pl.semaphore_signal(bar, inc=1, device_id={"patch": q}, device_id_type=MESH_ID)
    pl.semaphore_wait(bar, len(peers) + 1)

    order = sorted(range(1, hi), key=lambda j: -min(j, hi - j))
    near = order[::-1]
    xc, za, zb, ya, yb = {}, {}, {}, {}, {}

    def open_x(q):
        xc[q] = go(source(q), row(h, lo, q), xsem, q, xnb)

    def open_rest(q):
        for j in order:
            za[q, j] = go(source(q), row(h, lo, q), zsem, 2 * hi * q + j, zpeer[j])
        ya[q, 0] = go(source(q), row(h, lo, q), ysem, 2 * hi * q, ynb)

    def side(q):
        xc[q].wait_recv()
        part = row(h, lox, q)
        for j in order:
            zb[q, j] = go(part, part, zsem, 2 * hi * q + hi + j, zpeer[j])
        yb[q, 0] = go(part, part, ysem, 2 * hi * q + hi, ynb)

    def relay(q, j):
        za[q, j].wait_recv()
        part = row((h + hi - j) % hi, lo, q)
        ya[q, j] = go(part, part, ysem, 2 * hi * q + j, ynb)

    def relay_side(q, j):
        zb[q, j].wait_recv()
        part = row((h + hi - j) % hi, lox, q)
        yb[q, j] = go(part, part, ysem, 2 * hi * q + hi + j, ynb)

    def arrive(q):
        for j in range(hi):
            ya[q, j].wait_recv()
            yb[q, j].wait_recv()

    open_x(0)
    open_rest(0)

    def hot(count, ids, dtype):
        iota = lax.broadcasted_iota(jnp.int32, (count, ids.shape[1]), 0)
        return jnp.where(iota == ids, 1.0, 0.0).astype(dtype)

    fetch[0].wait()
    fetch[1].wait()
    for d in range(2):
        sel[:, d * halo : (d + 1) * halo] = hot(vs, rows[d : d + 1], BF)
    parts = split3(restb[...])
    sent = sum(mm(part, sel[...]) for part in parts)
    rc = []
    for d in range(2):
        restx[d] = sent[:, d * halo : (d + 1) * halo]
    for i in range(2):
        rc.append(go(restx.at[slot[i]], restx.at[3 - slot[i]], rsem, i, toward[i]))

    hc, fc = {}, {}

    def part_of(ref, base, c, d):
        at = pl.multiple_of(base + d * halo + pos * hs, hs)
        return ref.at[c, pl.ds(at, hs)]

    def reach(c, i):
        hc[c, i] = go(
            part_of(hb, 0, c, slot[i]), part_of(be, vs, c, 1 - slot[i]),
            hsem, 2 * c + i, toward[i],
        )

    for c in range(3):
        fetch[2 + c].wait()
        hb[c] = mm(sel[...], be[c, 0:vs], TN).astype(BF)
        reach(c, 1)
        reach(c, 0)
        if c == 0:
            side(0)
            for q in range(1, CHUNKS):
                open_x(q)

    def swap(c, i):
        hc[c, i].wait_recv()
        part = part_of(be, vs, c, slot[i])
        fc[c, i] = cross(part, part, wsem, 2 * c + i)

    for f in fetch[5:]:
        f.wait()

    def corner(ref, i, at, count):
        return hot(ext, ref[i : i + 1, at : at + count], F32)

    def build(at, count, plus, minus):
        total = None
        for ref, i, begin in plus:
            one = corner(ref, i, begin, count)
            total = one if total is None else total + one
        for ref, i, begin in minus:
            total = total - corner(ref, i, begin, count)
        inc[:, at : at + count] = total.astype(BF)
        inct[at : at + count] = inc[:, at : at + count].T

    def build_edges(i):
        for b in range(0, nt, LANES):
            build(i * nt + b, LANES, [(tri, i + 1, b)], [(tri, i, b)])

    for j in near:
        relay(0, j)
    build_edges(0)
    for j in near:
        relay_side(0, j)
    for q in range(1, CHUNKS):
        open_rest(q)
        side(q)
    build_edges(1)
    for b in range(0, nh, LANES):
        build(
            2 * nt + b, LANES, [(hin, 2, b), (hin, 3, b)], [(hin, 0, b), (hin, 1, b)]
        )
    for i in range(2):
        swap(0, i)
    keep.wait()

    for i in range(3):
        sq[i] = column(rsq[i : i + 1])
        bd[i] = column(bend[i : i + 1])
    mb[...] = column(mass[...])
    for d in range(2):
        rc[d].wait_recv()
    for c in range(3):
        line = jnp.concatenate(
            [restb[c : c + 1], restx[2, c : c + 1], restx[3, c : c + 1]], axis=1
        )
        cols = sum(
            mm(inct[...], jnp.broadcast_to(part, (LANES, ext)), NT) for part in split3(line)
        )
        rb[c, 0 : 2 * nt] = cols[0 : 2 * nt]
        rb[c, 2 * nt :] = cols[2 * nt :] - bd[c]
    for c in range(3):
        bet[:, c * ext : c * ext + vs] = be[c, 0:vs].T

    def decode(c, at, count, lanes):
        here = pl.ds(at, count)
        dec[c, here, lanes] = mm(be[c, here], xs[:, lanes]).astype(BF)

    def stretch(c, lanes):
        for r in range(0, 2 * nt + nh, 352):
            edge[c, r : r + 352, lanes] = mm(inct[r : r + 352], dec[c, :, lanes])

    def prepare(q):
        lanes = pl.ds(q * pc, pc)
        arrive(q)
        for c in range(3):
            decode(c, 0, vs, lanes)
        for c in range(2):
            if q == 0:
                if c:
                    for i in range(2):
                        swap(c, i)
                for i in range(2):
                    fc[c, i].wait_recv()
            decode(c, vs, 2 * halo, lanes)
            stretch(c, lanes)

    prepare(0)
    for c in range(2):
        bet[:, c * ext + vs : (c + 1) * ext] = be[c, vs:ext].T
    for q in range(1, CHUNKS):
        for j in near:
            relay(q, j)
            relay_side(q, j)
    for i in range(2):
        swap(2, i)
    for i in range(2):
        fc[2, i].wait_recv()

    k = 4.0 * MEMBRANE / frames
    kc, yc, pcs = {}, {}, {}

    def elastic(q):
        step = 16

        def body(i, carry):
            r = pl.multiple_of(i * step, step)
            for t in range(0, pc, LANES):
                lanes = pl.ds(q * pc + t, LANES)
                e1 = [edge[c, pl.ds(r, step), lanes] + rb[c, pl.ds(r, step)] for c in range(3)]
                r2 = pl.multiple_of(nt + r, step)
                e2 = [edge[c, pl.ds(r2, step), lanes] + rb[c, pl.ds(r2, step)] for c in range(3)]
                e3 = [a + b for a, b in zip(e1, e2)]

                def strain(e, i):
                    return e[0] * e[0] + e[1] * e[1] + e[2] * e[2] - sq[i, pl.ds(r, step)]

                s1, s2, s3 = strain(e1, 0), strain(e2, 1), strain(e3, 2)
                for c in range(3):
                    u = s3 * e3[c]
                    force[c, pl.ds(r, step), pl.ds(t, LANES)] = (s1 * e1[c] + u).astype(BF)
                    force[c, pl.ds(r2, step), pl.ds(t, LANES)] = (s2 * e2[c] + u).astype(BF)
            return carry

        lax.fori_loop(0, nt // step, body, 0)

        def bend_body(i, carry):
            r = pl.multiple_of(2 * nt + i * step, step)
            for c in range(3):
                for t in range(0, pc, LANES):
                    e = edge[c, pl.ds(r, step), pl.ds(q * pc + t, LANES)] + rb[c, pl.ds(r, step)]
                    force[c, pl.ds(r, step), pl.ds(t, LANES)] = (
                        e * (0.5 * BENDING / MEMBRANE)
                    ).astype(BF)
            return carry

        lax.fori_loop(0, nh // step, bend_body, 0)

    def back(q, c, i):
        at = pl.multiple_of(c * ext + vs + slot[i] * halo, halo)
        to = pl.multiple_of((1 - slot[i]) * halo, halo)
        kc[q, c, i] = go(
            adj.at[q, pl.ds(at, halo)], bk.at[q, c, pl.ds(to, halo)],
            ksem, (q * 3 + c) * 2 + i, toward[i],
        )

    for q in range(CHUNKS):
        lanes = pl.ds(q * pc, pc)
        if q:
            prepare(q)
        decode(2, vs, 2 * halo, lanes)
        stretch(2, lanes)
        elastic(q)
        for c in range(3):
            adj[q, c * ext + vs : (c + 1) * ext] = (mm(inc[vs:ext], force[c]) * k).astype(BF)
            back(q, c, 1)
            back(q, c, 0)
        if q == CHUNKS - 1:
            oc = cross(xs, xo, osem, 0)
        for c in range(3):
            part = mm(inc[0:vs], force[c]) * k
            if c == 2:
                lift = mb[...] * (GRAVITY / frames)
                part = part + jnp.concatenate([lift] * (pc // LANES), axis=1)
            own[q, c] = part
            adj[q, c * ext : c * ext + vs] = part.astype(BF)
        if q == 0:
            bet[:, 2 * ext + vs : 3 * ext] = be[2, vs:ext].T
        for j in order + [0]:
            hh = (h + j) % hi
            here = pl.ds(pl.multiple_of(hh * PLANE * w, PLANE * w), PLANE * w)
            g[q, here] = mm(bet[here], adj[q]).astype(BF)
            for i, ll in enumerate((loy, lod)):
                at = pl.multiple_of((hh * PLANE + ll) * w, w)
                yc[q, j, i] = go(
                    g.at[q, pl.ds(at, w)], yl.at[q, j, i], ry, (q * hi + j) * 2 + i, ynb
                )

    def fold(q, j, i):
        hh = (h + j) % hi
        at = pl.multiple_of((hh * PLANE + (lox if i else lo)) * w, w)
        yc[q, j, i].wait_recv()
        return g[q, pl.ds(at, w)].astype(F32) + yl[q, j, i].astype(F32)

    zc = {}

    def depth(q):
        for j in order:
            for i in range(2):
                ysum[q, j, i] = fold(q, j, i).astype(BF)
                zc[q, j, i] = go(
                    ysum.at[q, j, i], zl.at[q, j, i], rz, (q * hi + j) * 2 + i, zpeer[j]
                )

    held = {}

    def gather_z(q, i):
        s = fold(q, 0, i)
        for j in order:
            zc[q, j, i].wait_recv()
            s = s + zl[q, j, i].astype(F32)
        return s

    def collect(q):
        for c in range(3):
            kc[q, c, 0].wait_recv()
            kc[q, c, 1].wait_recv()
            tot[c, :, q * pc : (q + 1) * pc] = (own[q, c] + mm(sel[...], bk[q, c])).astype(BF)
            theirs = pl.ds(pl.multiple_of((1 - pos) * half, half), half)
            pcs[q, c] = cross(
                tot.at[c, theirs, pl.ds(q * pc, pc)], got.at[c, :, pl.ds(q * pc, pc)],
                psem, q * 3 + c,
            )

    rxc = {}

    def turn(q):
        xsum[q] = gather_z(q, 1).astype(BF)
        rxc[q] = go(xsum.at[q], xl.at[q], rx, q, xnb)

    def finish(q):
        s = gather_z(q, 0)
        rxc[q].wait_recv()
        lg_ref[0, :, q * pc : (q + 1) * pc] = s
        lg_ref[1, :, q * pc : (q + 1) * pc] = xl[q].astype(F32)

    def product(which, src, lat, c):
        for r in range(0, kk, tile):
            bg_ref[which, c, :, r : r + tile] = mm(src, lat[r : r + tile], NT).astype(BF)

    for q in range(CHUNKS):
        depth(q)
    for q in range(CHUNKS - 1):
        collect(q)
    for q in range(CHUNKS):
        turn(q)
    collect(CHUNKS - 1)
    for c in range(3):
        product(0, tot[c, pl.ds(pl.multiple_of(pos * half, half), half)], xs, c)
    oc.wait_recv()
    for c in range(3):
        for q in range(CHUNKS):
            pcs[q, c].wait_recv()
        product(1, got[c], xo, c)
    for q in range(CHUNKS):
        finish(q)
    for c in out:
        c.wait_send()


def local(basis, latents, rest_pos, triangles, hinges, rest_sq, bend_rest, masses, send_rows):
    vs, kk = basis.shape[1:]
    ff, w = latents.shape
    halo = send_rows.shape[1]
    nt, nh = triangles.shape[1], hinges.shape[1]
    n = lax.axis_size("patch")
    hi = n // PLANE
    frames = ff * lax.axis_size("frame")
    ext = vs + 2 * halo
    ne = 2 * nt + nh
    pc = ff // CHUNKS
    v = pltpu.VMEM
    i32 = jnp.int32
    vm = pl.BlockSpec(memory_space=pltpu.VMEM)
    hbm = pl.BlockSpec(memory_space=pltpu.HBM)
    halves, lg = pl.pallas_call(
        functools.partial(kernel, n, frames),
        out_shape=[
            jax.ShapeDtypeStruct((2, 3, vs // 2, kk), BF),
            jax.ShapeDtypeStruct((2, w, ff), F32),
        ],
        in_specs=[hbm] * 9,
        out_specs=[vm] * 2,
        scratch_shapes=[
            v((kk, ff), BF),
            v((kk, ff), BF),
            v((3, ext, kk), BF),
            v((kk, 3 * ext), BF),
            v((3, 2 * halo, kk), BF),
            v((3, nt), i32),
            v((4, nh), i32),
            v((3, nt), F32),
            v((3, nh), F32),
            v((1, vs), F32),
            v((2, halo), i32),
            v((3, vs), F32),
            v((4, 3, halo), F32),
            v((vs, 2 * halo), BF),
            v((ext, ne), BF),
            v((ne, ext), BF),
            v((3, ne, LANES), F32),
            v((3, nt, LANES), F32),
            v((3, nh, LANES), F32),
            v((vs, LANES), F32),
            v((3, ext, ff), BF),
            v((3, ne, ff), F32),
            v((3, ne, pc), BF),
            v((CHUNKS, 3 * ext, pc), BF),
            v((CHUNKS, 3, vs, pc), F32),
            v((CHUNKS, 3, 2 * halo, pc), BF),
            v((3, vs, ff), BF),
            v((3, vs // 2, ff), BF),
            v((CHUNKS, kk, pc), BF),
            v((CHUNKS, hi, 2, w, pc), BF),
            v((CHUNKS, hi, 2, w, pc), BF),
            v((CHUNKS, hi, 2, w, pc), BF),
            v((CHUNKS, w, pc), BF),
            v((CHUNKS, w, pc), BF),
            DMA((11,)),
            DMA((2, CHUNKS)),
            DMA((2, CHUNKS * 2 * hi)),
            DMA((2, CHUNKS * 2 * hi)),
            DMA((2, 2)),
            DMA((2, 6)),
            DMA((2, 6)),
            DMA((2, 1)),
            DMA((2, CHUNKS * 6)),
            DMA((2, CHUNKS * 3)),
            DMA((2, CHUNKS * hi * 2)),
            DMA((2, CHUNKS * hi * 2)),
            DMA((2, CHUNKS)),
        ],
        compiler_params=pltpu.CompilerParams(
            collective_id=0, has_side_effects=True, vmem_limit_bytes=52000 * 1024
        ),
    )(
        *(
            pltpu.with_memory_space_constraint(a, pltpu.HBM)
            for a in (
                latents.T, basis, rest_pos, triangles, hinges, rest_sq, bend_rest,
                masses.reshape(1, vs), send_rows,
            )
        )
    )
    return (halves[0].astype(F32) + halves[1].astype(F32), (lg[0] + lg[1]).T)


def solution(mesh):
    return jax.shard_map(
        local,
        mesh=mesh,
        in_specs=(
            P(None, "patch", None),
            P("frame", "patch"),
            P(None, "patch"),
            P(None, "patch"),
            P(None, "patch"),
            P(None, "patch"),
            P(None, "patch"),
            P("patch"),
            P(None, "patch"),
        ),
        out_specs=(P(None, ("patch", "frame"), None), P("frame", "patch")),
        check_vma=False,
    )
```

```python
import functools

import jax
import jax.numpy as jnp
from jax import lax
from jax.experimental import pallas as pl
from jax.experimental.pallas import tpu as pltpu
from jax.sharding import PartitionSpec as P

MEMBRANE = 5.0
BENDING = 5.0
GRAVITY = 40.0
BF = jnp.bfloat16
F32 = jnp.float32
PLANE = 4
LANES = 128
CHUNKS = 2
MESH_ID = pl.DeviceIdType.MESH
DMA = pltpu.SemaphoreType.DMA


def mm(a, b, dims=((1,), (0,))):
    return lax.dot_general(a, b, (dims, ((), ())), preferred_element_type=F32)


NT = ((1,), (1,))
TN = ((0,), (0,))


def split3(r):
    hi = r.astype(BF)
    left = r - hi.astype(F32)
    mid = left.astype(BF)
    return hi, mid, (left - mid.astype(F32)).astype(BF)


def send(src, dst, ss, rs, q):
    return pltpu.make_async_remote_copy(
        src_ref=src, dst_ref=dst, send_sem=ss, recv_sem=rs,
        device_id={"patch": q}, device_id_type=MESH_ID,
    )


def column(row):
    return jnp.broadcast_to(row, (LANES, row.shape[1])).T


def kernel(
    n, frames,
    x_hbm, b_hbm, rest_hbm, tri_hbm, hin_hbm, rsq_hbm, bend_hbm, mass_hbm, rows_hbm,
    bg_ref, lg_ref,
    xs, xo, be, bet, hb, tri, hin, rsq, bend, mass, rows, restb, restx, sel, inc, inct,
    rb, sq, bd, mb, dec, edge, force, adj, own, bk, tot, got, g, yl, ysum, zl, xsum, xl,
    ins, xsem, ysem, zsem, rsem, hsem, wsem, osem, ksem, psem, ry, rz, rx,
):
    hi = n // PLANE
    w = x_hbm.shape[0]
    p = lax.axis_index("patch")
    pos = lax.axis_index("frame")
    h, lo = p // PLANE, p % PLANE
    xnb = p + 1 - 2 * (p % 2)
    ynb = p + 2 - 4 * ((p // 2) % 2)
    lox, loy, lod = xnb % PLANE, ynb % PLANE, PLANE - 1 - lo
    odd = p % 2
    toward = [xnb, (p + n - 1 + 2 * odd) % n]
    slot = [1 - odd, odd]
    ring = [(p + n - 1) % n, (p + 1) % n]
    vs, kk = b_hbm.shape[1:]
    ff = x_hbm.shape[1]
    halo = rows_hbm.shape[1]
    ext = vs + 2 * halo
    hs = halo // 2
    nt, nh = tri_hbm.shape[1], hin_hbm.shape[1]
    half = vs // 2
    pc = ff // CHUNKS
    tile = 256

    def partner(src, dst, sems, at):
        return pltpu.make_async_remote_copy(
            src_ref=src, dst_ref=dst, send_sem=sems.at[0, at], recv_sem=sems.at[1, at],
            device_id={"frame": 1 - pos}, device_id_type=MESH_ID,
        )

    out = []

    def go(src, dst, sems, at, q):
        c = send(src, dst, sems.at[0, at], sems.at[1, at], q)
        c.start()
        out.append(c)
        return c

    def cross(src, dst, sems, at):
        c = partner(src, dst, sems, at)
        c.start()
        out.append(c)
        return c

    small = [(rows_hbm, rows), (rest_hbm, restb), (tri_hbm, tri), (hin_hbm, hin),
             (rsq_hbm, rsq), (bend_hbm, bend), (mass_hbm, mass)]
    ends = [(s, d) for s, d in small[:2]]
    ends += [(b_hbm.at[c], be.at[c, pl.ds(0, vs)]) for c in range(3)]
    ends += small[2:]
    fetch = [pltpu.make_async_copy(s, d, ins.at[i]) for i, (s, d) in enumerate(ends)]
    for f in fetch:
        f.start()

    zpeer = [((h + j) % hi) * PLANE + lo for j in range(hi)]

    def row(hh, ll, q):
        at = pl.multiple_of((hh * PLANE + ll) * w, w)
        return xs.at[pl.ds(at, w), pl.ds(q * pc, pc)]

    def source(q):
        return x_hbm.at[:, pl.ds(q * pc, pc)]

    keep = pltpu.make_async_copy(
        x_hbm, xs.at[pl.ds(pl.multiple_of(p * w, w), w)], ins.at[len(ends)]
    )
    keep.start()

    bar = pltpu.get_barrier_semaphore()
    pl.semaphore_signal(bar, inc=1, device_id={"frame": 1 - pos}, device_id_type=MESH_ID)
    peers = zpeer[1:] + [xnb, ynb] + ring
    for q in peers:
        pl.semaphore_signal(bar, inc=1, device_id={"patch": q}, device_id_type=MESH_ID)
    pl.semaphore_wait(bar, len(peers) + 1)

    order = sorted(range(1, hi), key=lambda j: -min(j, hi - j))
    near = order[::-1]
    xc, za, zb, ya, yb = {}, {}, {}, {}, {}

    def open_x(q):
        xc[q] = go(source(q), row(h, lo, q), xsem, q, xnb)

    def open_rest(q):
        for j in order:
            za[q, j] = go(source(q), row(h, lo, q), zsem, 2 * hi * q + j, zpeer[j])
        ya[q, 0] = go(source(q), row(h, lo, q), ysem, 2 * hi * q, ynb)

    def side(q):
        xc[q].wait_recv()
        part = row(h, lox, q)
        for j in order:
            zb[q, j] = go(part, part, zsem, 2 * hi * q + hi + j, zpeer[j])
        yb[q, 0] = go(part, part, ysem, 2 * hi * q + hi, ynb)

    def relay(q, j):
        za[q, j].wait_recv()
        part = row((h + hi - j) % hi, lo, q)
        ya[q, j] = go(part, part, ysem, 2 * hi * q + j, ynb)

    def relay_side(q, j):
        zb[q, j].wait_recv()
        part = row((h + hi - j) % hi, lox, q)
        yb[q, j] = go(part, part, ysem, 2 * hi * q + hi + j, ynb)

    def arrive(q):
        for j in range(hi):
            ya[q, j].wait_recv()
            yb[q, j].wait_recv()

    open_x(0)
    open_rest(0)

    def hot(count, ids, dtype):
        iota = lax.broadcasted_iota(jnp.int32, (count, ids.shape[1]), 0)
        return jnp.where(iota == ids, 1.0, 0.0).astype(dtype)

    fetch[0].wait()
    fetch[1].wait()
    for d in range(2):
        sel[:, d * halo : (d + 1) * halo] = hot(vs, rows[d : d + 1], BF)
    parts = split3(restb[...])
    sent = sum(mm(part, sel[...]) for part in parts)
    rc = []
    for d in range(2):
        restx[d] = sent[:, d * halo : (d + 1) * halo]
    for i in range(2):
        rc.append(go(restx.at[slot[i]], restx.at[3 - slot[i]], rsem, i, toward[i]))

    hc, fc = {}, {}

    def part_of(ref, base, c, d):
        at = pl.multiple_of(base + d * halo + pos * hs, hs)
        return ref.at[c, pl.ds(at, hs)]

    def reach(c, i):
        hc[c, i] = go(
            part_of(hb, 0, c, slot[i]), part_of(be, vs, c, 1 - slot[i]),
            hsem, 2 * c + i, toward[i],
        )

    for c in range(3):
        fetch[2 + c].wait()
        hb[c] = mm(sel[...], be[c, 0:vs], TN).astype(BF)
        reach(c, 1)
        reach(c, 0)
        if c == 0:
            side(0)
            for q in range(1, CHUNKS):
                open_x(q)

    def swap(c, i):
        hc[c, i].wait_recv()
        part = part_of(be, vs, c, slot[i])
        fc[c, i] = cross(part, part, wsem, 2 * c + i)

    for f in fetch[5:]:
        f.wait()

    def corner(ref, i, at, count):
        return hot(ext, ref[i : i + 1, at : at + count], F32)

    def build(at, count, plus, minus):
        total = None
        for ref, i, begin in plus:
            one = corner(ref, i, begin, count)
            total = one if total is None else total + one
        for ref, i, begin in minus:
            total = total - corner(ref, i, begin, count)
        inc[:, at : at + count] = total.astype(BF)
        inct[at : at + count] = inc[:, at : at + count].T

    def build_edges(i):
        for b in range(0, nt, LANES):
            build(i * nt + b, LANES, [(tri, i + 1, b)], [(tri, i, b)])

    for j in near:
        relay(0, j)
    build_edges(0)
    for j in near:
        relay_side(0, j)
    for q in range(1, CHUNKS):
        open_rest(q)
        side(q)
    build_edges(1)
    for b in range(0, nh, LANES):
        build(
            2 * nt + b, LANES, [(hin, 2, b), (hin, 3, b)], [(hin, 0, b), (hin, 1, b)]
        )
    for i in range(2):
        swap(0, i)
    keep.wait()

    for i in range(3):
        sq[i] = column(rsq[i : i + 1])
        bd[i] = column(bend[i : i + 1])
    mb[...] = column(mass[...])
    for d in range(2):
        rc[d].wait_recv()
    for c in range(3):
        line = jnp.concatenate(
            [restb[c : c + 1], restx[2, c : c + 1], restx[3, c : c + 1]], axis=1
        )
        cols = sum(
            mm(inct[...], jnp.broadcast_to(part, (LANES, ext)), NT) for part in split3(line)
        )
        rb[c, 0 : 2 * nt] = cols[0 : 2 * nt]
        rb[c, 2 * nt :] = cols[2 * nt :] - bd[c]
    for c in range(3):
        bet[:, c * ext : c * ext + vs] = be[c, 0:vs].T

    def decode(c, at, count, lanes):
        here = pl.ds(at, count)
        dec[c, here, lanes] = mm(be[c, here], xs[:, lanes]).astype(BF)

    def stretch(c, lanes):
        for r in range(0, 2 * nt + nh, 352):
            edge[c, r : r + 352, lanes] = mm(inct[r : r + 352], dec[c, :, lanes])

    def prepare(q):
        lanes = pl.ds(q * pc, pc)
        arrive(q)
        for c in range(3):
            decode(c, 0, vs, lanes)
        for c in range(2):
            if q == 0:
                if c:
                    for i in range(2):
                        swap(c, i)
                for i in range(2):
                    fc[c, i].wait_recv()
            decode(c, vs, 2 * halo, lanes)
            stretch(c, lanes)

    for q in range(1, CHUNKS):
        for j in near:
            relay(q, j)
            relay_side(q, j)
    prepare(0)
    for c in range(2):
        bet[:, c * ext + vs : (c + 1) * ext] = be[c, vs:ext].T
    for i in range(2):
        swap(2, i)
    for i in range(2):
        fc[2, i].wait_recv()

    k = 4.0 * MEMBRANE / frames
    kc, yc, pcs = {}, {}, {}

    def elastic(q):
        step = 16

        def body(i, carry):
            r = pl.multiple_of(i * step, step)
            for t in range(0, pc, LANES):
                lanes = pl.ds(q * pc + t, LANES)
                e1 = [edge[c, pl.ds(r, step), lanes] + rb[c, pl.ds(r, step)] for c in range(3)]
                r2 = pl.multiple_of(nt + r, step)
                e2 = [edge[c, pl.ds(r2, step), lanes] + rb[c, pl.ds(r2, step)] for c in range(3)]
                e3 = [a + b for a, b in zip(e1, e2)]

                def strain(e, i):
                    return e[0] * e[0] + e[1] * e[1] + e[2] * e[2] - sq[i, pl.ds(r, step)]

                s1, s2, s3 = strain(e1, 0), strain(e2, 1), strain(e3, 2)
                for c in range(3):
                    u = s3 * e3[c]
                    force[c, pl.ds(r, step), pl.ds(t, LANES)] = (s1 * e1[c] + u).astype(BF)
                    force[c, pl.ds(r2, step), pl.ds(t, LANES)] = (s2 * e2[c] + u).astype(BF)
            return carry

        lax.fori_loop(0, nt // step, body, 0, unroll=4)

        def bend_body(i, carry):
            r = pl.multiple_of(2 * nt + i * step, step)
            for c in range(3):
                for t in range(0, pc, LANES):
                    e = edge[c, pl.ds(r, step), pl.ds(q * pc + t, LANES)] + rb[c, pl.ds(r, step)]
                    force[c, pl.ds(r, step), pl.ds(t, LANES)] = (
                        e * (0.5 * BENDING / MEMBRANE)
                    ).astype(BF)
            return carry

        lax.fori_loop(0, nh // step, bend_body, 0, unroll=4)

    def back(q, c, i):
        at = pl.multiple_of(c * ext + vs + slot[i] * halo, halo)
        to = pl.multiple_of((1 - slot[i]) * halo, halo)
        kc[q, c, i] = go(
            adj.at[q, pl.ds(at, halo)], bk.at[q, c, pl.ds(to, halo)],
            ksem, (q * 3 + c) * 2 + i, toward[i],
        )

    for q in range(CHUNKS):
        lanes = pl.ds(q * pc, pc)
        if q:
            prepare(q)
        decode(2, vs, 2 * halo, lanes)
        stretch(2, lanes)
        elastic(q)
        for c in range(3):
            adj[q, c * ext + vs : (c + 1) * ext] = (mm(inc[vs:ext], force[c]) * k).astype(BF)
            back(q, c, 1)
            back(q, c, 0)
        if q == CHUNKS - 1:
            oc = cross(xs, xo, osem, 0)
        for c in range(3):
            part = mm(inc[0:vs], force[c]) * k
            if c == 2:
                lift = mb[...] * (GRAVITY / frames)
                part = part + jnp.concatenate([lift] * (pc // LANES), axis=1)
            own[q, c] = part
            adj[q, c * ext : c * ext + vs] = part.astype(BF)
        if q == 0:
            bet[:, 2 * ext + vs : 3 * ext] = be[2, vs:ext].T
        for j in order + [0]:
            hh = (h + j) % hi
            here = pl.ds(pl.multiple_of(hh * PLANE * w, PLANE * w), PLANE * w)
            g[q, here] = mm(bet[here], adj[q]).astype(BF)
            for i, ll in enumerate((loy, lod)):
                at = pl.multiple_of((hh * PLANE + ll) * w, w)
                yc[q, j, i] = go(
                    g.at[q, pl.ds(at, w)], yl.at[q, j, i], ry, (q * hi + j) * 2 + i, ynb
                )

    def fold(q, j, i):
        hh = (h + j) % hi
        at = pl.multiple_of((hh * PLANE + (lox if i else lo)) * w, w)
        yc[q, j, i].wait_recv()
        return g[q, pl.ds(at, w)].astype(F32) + yl[q, j, i].astype(F32)

    zc = {}

    def depth(q):
        for j in order:
            for i in range(2):
                ysum[q, j, i] = fold(q, j, i).astype(BF)
                zc[q, j, i] = go(
                    ysum.at[q, j, i], zl.at[q, j, i], rz, (q * hi + j) * 2 + i, zpeer[j]
                )

    held = {}

    def gather_z(q, i):
        s = fold(q, 0, i)
        for j in order:
            zc[q, j, i].wait_recv()
            s = s + zl[q, j, i].astype(F32)
        return s

    def collect(q):
        for c in range(3):
            kc[q, c, 0].wait_recv()
            kc[q, c, 1].wait_recv()
            tot[c, :, q * pc : (q + 1) * pc] = (own[q, c] + mm(sel[...], bk[q, c])).astype(BF)
            theirs = pl.ds(pl.multiple_of((1 - pos) * half, half), half)
            pcs[q, c] = cross(
                tot.at[c, theirs, pl.ds(q * pc, pc)], got.at[c, :, pl.ds(q * pc, pc)],
                psem, q * 3 + c,
            )

    rxc = {}

    def turn(q):
        xsum[q] = gather_z(q, 1).astype(BF)
        rxc[q] = go(xsum.at[q], xl.at[q], rx, q, xnb)

    def finish(q):
        s = gather_z(q, 0)
        rxc[q].wait_recv()
        lg_ref[0, :, q * pc : (q + 1) * pc] = s
        lg_ref[1, :, q * pc : (q + 1) * pc] = xl[q].astype(F32)

    def product(which, src, lat, c):
        for r in range(0, kk, tile):
            bg_ref[which, c, :, r : r + tile] = mm(src, lat[r : r + tile], NT).astype(BF)

    for q in range(CHUNKS):
        depth(q)
    for q in range(CHUNKS - 1):
        collect(q)
    for q in range(CHUNKS):
        turn(q)
    collect(CHUNKS - 1)
    for c in range(3):
        product(0, tot[c, pl.ds(pl.multiple_of(pos * half, half), half)], xs, c)
    oc.wait_recv()
    for c in range(3):
        for q in range(CHUNKS):
            pcs[q, c].wait_recv()
        product(1, got[c], xo, c)
    for q in range(CHUNKS):
        finish(q)
    for c in out:
        c.wait_send()


def local(basis, latents, rest_pos, triangles, hinges, rest_sq, bend_rest, masses, send_rows):
    vs, kk = basis.shape[1:]
    ff, w = latents.shape
    halo = send_rows.shape[1]
    nt, nh = triangles.shape[1], hinges.shape[1]
    n = lax.axis_size("patch")
    hi = n // PLANE
    frames = ff * lax.axis_size("frame")
    ext = vs + 2 * halo
    ne = 2 * nt + nh
    pc = ff // CHUNKS
    v = pltpu.VMEM
    i32 = jnp.int32
    vm = pl.BlockSpec(memory_space=pltpu.VMEM)
    hbm = pl.BlockSpec(memory_space=pltpu.HBM)
    halves, lg = pl.pallas_call(
        functools.partial(kernel, n, frames),
        out_shape=[
            jax.ShapeDtypeStruct((2, 3, vs // 2, kk), BF),
            jax.ShapeDtypeStruct((2, w, ff), F32),
        ],
        in_specs=[hbm] * 9,
        out_specs=[vm] * 2,
        scratch_shapes=[
            v((kk, ff), BF),
            v((kk, ff), BF),
            v((3, ext, kk), BF),
            v((kk, 3 * ext), BF),
            v((3, 2 * halo, kk), BF),
            v((3, nt), i32),
            v((4, nh), i32),
            v((3, nt), F32),
            v((3, nh), F32),
            v((1, vs), F32),
            v((2, halo), i32),
            v((3, vs), F32),
            v((4, 3, halo), F32),
            v((vs, 2 * halo), BF),
            v((ext, ne), BF),
            v((ne, ext), BF),
            v((3, ne, LANES), F32),
            v((3, nt, LANES), F32),
            v((3, nh, LANES), F32),
            v((vs, LANES), F32),
            v((3, ext, ff), BF),
            v((3, ne, ff), F32),
            v((3, ne, pc), BF),
            v((CHUNKS, 3 * ext, pc), BF),
            v((CHUNKS, 3, vs, pc), F32),
            v((CHUNKS, 3, 2 * halo, pc), BF),
            v((3, vs, ff), BF),
            v((3, vs // 2, ff), BF),
            v((CHUNKS, kk, pc), BF),
            v((CHUNKS, hi, 2, w, pc), BF),
            v((CHUNKS, hi, 2, w, pc), BF),
            v((CHUNKS, hi, 2, w, pc), BF),
            v((CHUNKS, w, pc), BF),
            v((CHUNKS, w, pc), BF),
            DMA((11,)),
            DMA((2, CHUNKS)),
            DMA((2, CHUNKS * 2 * hi)),
            DMA((2, CHUNKS * 2 * hi)),
            DMA((2, 2)),
            DMA((2, 6)),
            DMA((2, 6)),
            DMA((2, 1)),
            DMA((2, CHUNKS * 6)),
            DMA((2, CHUNKS * 3)),
            DMA((2, CHUNKS * hi * 2)),
            DMA((2, CHUNKS * hi * 2)),
            DMA((2, CHUNKS)),
        ],
        compiler_params=pltpu.CompilerParams(
            collective_id=0, has_side_effects=True, vmem_limit_bytes=52000 * 1024
        ),
    )(
        *(
            pltpu.with_memory_space_constraint(a, pltpu.HBM)
            for a in (
                latents.T, basis, rest_pos, triangles, hinges, rest_sq, bend_rest,
                masses.reshape(1, vs), send_rows,
            )
        )
    )
    return (halves[0].astype(F32) + halves[1].astype(F32), (lg[0] + lg[1]).T)


def solution(mesh):
    return jax.shard_map(
        local,
        mesh=mesh,
        in_specs=(
            P(None, "patch", None),
            P("frame", "patch"),
            P(None, "patch"),
            P(None, "patch"),
            P(None, "patch"),
            P(None, "patch"),
            P(None, "patch"),
            P("patch"),
            P(None, "patch"),
        ),
        out_specs=(P(None, ("patch", "frame"), None), P("frame", "patch")),
        check_vma=False,
    )
```
